512 devices in a mesh: pt: 64 (over x, z, core), dir: 8 (over y).
Axes of the slice: x: 4, y: 8, z: 8, core: 2. Of those that a mesh axis runs over, the one named last changes fastest.
Arguments:
- axial: float32 [65536], P('pt'), may hold values from 0.1 to 0.3
- thrust_weight: float32 [8, 16, 65536], P('dir', None, 'pt'), may hold values from 0.5 to 2
- xdown: float32 [8, 65536], P('dir', 'pt'), may hold values from 0 to 40
- ycross: float32 [8, 65536], P('dir', 'pt'), may hold values from 0 to 4
- freq: float32 [8, 16], P('dir'), may hold values from 0.005 to 0.05
- upstream: int32 [8, 512, 16], P('dir', 'pt'), may hold values from 0 to 511, as said below
- counts: int32 [8, 512], P('dir', 'pt'), may hold values from 1 to 16
Outputs:
- power: float32 [8, 16, 65536], P('dir', None, 'pt')
- grad_axial: float32 [65536], P('pt')
The draws below stay inside these ranges and needn't reach their ends.
Inputs may be any that keep to these rules, and one draw needn't show every extreme that they name: `upstream`: for each direction and target block the entries name distinct blocks, each owned by an index of pt at most 3 from the target block's owner; only the first counts entries are used. In each direction some target block uses blocks exactly 3 owners away on both sides.
All inputs are finite; a program needn't handle non-finite values.
Results may differ from the reference program's by a relative error of at most 0.0004.
Values sent between devices are 32-bit elements; how exact they have to be, the bound alone decides.
No kernel may reach another device: no remote copies, remote signals or barrier semaphores. Data moves between devices by JAX's collectives and lax.ppermute only.
A program may use at most 64 MiB of HBM per device.

```python
import math
import jax
import jax.numpy as jnp
from jax import lax

BLOCK = 128
BLK_DEV = 8
GRID = 5
SPEEDS = 16
PAIRS = 16
REACH = 3
DIRS = 8
NBLK = 512
NTURB = 65536
N_PT = 64


def band_first(key):
    return jax.random.randint(jax.random.fold_in(key, 11), (DIRS,), REACH, N_PT - REACH)


def draw_counts(key, part):
    band_start = band_first(key)
    blocks = jnp.arange(NBLK, dtype=jnp.int32)
    owner_of = blocks // BLK_DEV
    inside = (owner_of[None, :] - band_start[:, None]) % N_PT < max(N_PT // 4, 1)
    random_bits = jax.random.randint(jax.random.fold_in(key, 12), (DIRS, NBLK), 0, 1 << 20)
    heavy_count = 1 + random_bits % PAIRS
    light_count = 1 + random_bits % max(PAIRS // 4, 1)
    result = jnp.where(inside, heavy_count, light_count)
    forced = blocks[None, :] == (band_start * BLK_DEV)[:, None]
    return jnp.where(forced, PAIRS, result).astype(jnp.int32)


def draw_upstream(key, part):
    band_start = band_first(key)
    blocks = jnp.arange(NBLK, dtype=jnp.int32)
    owner_of = blocks // BLK_DEV
    owner_gap = owner_of[None, :] - owner_of[:, None]
    allowed = jnp.abs(owner_gap) <= REACH
    random_bits = jax.random.randint(jax.random.fold_in(key, 21), (DIRS, NBLK, NBLK), 0, 1 << 20)
    scores = random_bits * NBLK + blocks[None, None, :]
    forced_target = blocks[None, :, None] == (band_start * BLK_DEV)[:, None, None]
    lower_pick = blocks[None, None, :] == ((band_start - REACH) * BLK_DEV)[:, None, None]
    upper_pick = blocks[None, None, :] == ((band_start + REACH) * BLK_DEV)[:, None, None]
    scores = jnp.where(forced_target & (lower_pick | upper_pick), scores + (1 << 30), scores)
    scores = jnp.where(allowed[None, :, :], scores, -1)
    chosen = lax.top_k(scores, PAIRS)[1]
    return chosen.astype(jnp.int32)


def block_levels(key, shape, shards, smallest, top_value):
    level = 1.0
    for dim, blocks in shards:
        heights = jax.random.uniform(jax.random.fold_in(jax.random.fold_in(key, 6), dim), (blocks,), jnp.float32, smallest / len(shards), top_value / len(shards))
        level = level * jnp.repeat(jnp.exp(heights), shape[dim] // blocks).reshape((-1,) + (1,) * (len(shape) - 1 - dim))
    return level


def setup_inputs(seed: int = 0) -> dict:
    arg_keys = jax.random.split(jax.random.key(seed), 8)
    return {
        "axial": jnp.clip(0.1 + 0.20000001043081284 * jax.random.uniform(arg_keys[0], (NTURB,), jnp.float32) ** block_levels(arg_keys[0], (NTURB,), ((0, 64),), -0.2, 0.2), 0.1, 0.3),
        "thrust_weight": jnp.clip(jnp.exp(math.log(2.0) - 1.3862944 * jax.random.uniform(arg_keys[1], (DIRS, SPEEDS, NTURB), jnp.float32) ** block_levels(arg_keys[1], (DIRS, SPEEDS, NTURB), ((0, 8), (2, 64)), -0.2, 0.2)), 0.5, 2.0),
        "xdown": jnp.clip(40.0 * jax.random.uniform(arg_keys[2], (DIRS, NTURB), jnp.float32) ** block_levels(arg_keys[2], (DIRS, NTURB), ((0, 8), (1, 64)), -0.2, 0.2), 0.0, 40.0),
        "ycross": jnp.clip(4.0 * jax.random.uniform(arg_keys[3], (DIRS, NTURB), jnp.float32) ** block_levels(arg_keys[3], (DIRS, NTURB), ((0, 8), (1, 64)), -0.2, 0.2), 0.0, 4.0),
        "freq": jnp.clip(jnp.exp(math.log(0.05) - 2.3025851 * jax.random.uniform(arg_keys[4], (DIRS, SPEEDS), jnp.float32) ** block_levels(arg_keys[4], (DIRS, SPEEDS), ((0, 8),), -0.2, 0.2)), 0.005, 0.05),
        "upstream": draw_upstream(jax.random.fold_in(arg_keys[7], 71), 0),
        "counts": draw_counts(jax.random.fold_in(arg_keys[7], 71), 0),
    }


SIGMA_ZERO = 0.5
EXPANSION = 0.03
STRENGTH_SCALE = 0.25
ROTOR_SPAN = 0.8


def rotor_points():
    points = jnp.arange(GRID * GRID, dtype=jnp.int32)
    across = ROTOR_SPAN * ((points % GRID).astype(jnp.float32) / (GRID - 1) - 0.5)
    upward = ROTOR_SPAN * ((points // GRID).astype(jnp.float32) / (GRID - 1) - 0.5)
    return across, upward


def wind_speeds():
    return 0.4 + 0.75 * jnp.arange(SPEEDS, dtype=jnp.float32) / (SPEEDS - 1)


def kernel_tile(target_x, target_y, source_x, source_y):
    across, upward = rotor_points()
    ahead_dist = jnp.maximum(target_x[None, None, :] - source_x[:, None, None], 0.0)
    spread_width = SIGMA_ZERO + EXPANSION * ahead_dist
    lateral = target_y[None, None, :] + across[None, :, None] - source_y[:, None, None]
    spread = lateral * lateral + (upward * upward)[None, :, None]
    width_ratio = SIGMA_ZERO / spread_width
    kernel = STRENGTH_SCALE * width_ratio * width_ratio * (1.0 - jnp.exp(-ahead_dist)) * jnp.exp(-spread / (2.0 * spread_width * spread_width))
    return kernel.reshape(source_x.shape[0], -1).astype(jnp.bfloat16)


def reference(axial, thrust_weight, xdown, ycross, freq, upstream, counts):
    speeds = wind_speeds()
    rotor_count = GRID * GRID
    power_coef = 4.0 * axial * (1.0 - axial) ** 2
    slope_coef = 4.0 * (1.0 - axial) * (1.0 - 3.0 * axial)
    total_turbines = axial.shape[0]
    block_total = total_turbines // BLOCK
    powers = []
    gradient = jnp.zeros((total_turbines,), jnp.float32)
    for direction in range(xdown.shape[0]):
        strength = (axial[None, :] * thrust_weight[direction]).astype(jnp.bfloat16)
        turbine_x = xdown[direction]
        turbine_y = ycross[direction]
        weights = freq[direction]

        def one_block(block_index, state_pair):
            cube_means, back_sum = state_pair
            first_turbine = (block_index * BLOCK).astype(jnp.int32)
            target_x = lax.dynamic_slice_in_dim(turbine_x, first_turbine, BLOCK)
            target_y = lax.dynamic_slice_in_dim(turbine_y, first_turbine, BLOCK)
            listed = upstream[direction, block_index]
            in_use = counts[direction, block_index]

            def tile_for_slot(slot_index):
                first_source = (listed[slot_index] * BLOCK).astype(jnp.int32)
                kernel = kernel_tile(target_x, target_y,
                                     lax.dynamic_slice_in_dim(turbine_x, first_source, BLOCK),
                                     lax.dynamic_slice_in_dim(turbine_y, first_source, BLOCK))
                return first_source, kernel

            def forward(slot_index, deficit):
                first_source, kernel = tile_for_slot(slot_index)
                source_block = lax.dynamic_slice_in_dim(strength, first_source, BLOCK, 1)
                return deficit + jnp.dot(source_block, kernel, preferred_element_type=jnp.float32)

            deficit = lax.fori_loop(0, in_use, forward, jnp.zeros((SPEEDS, rotor_count * BLOCK), jnp.float32))
            velocity = (speeds[:, None] / (1.0 + deficit)).reshape(SPEEDS, rotor_count, BLOCK)
            cube_mean = jnp.mean(velocity ** 3, axis=1)
            power_block = lax.dynamic_slice_in_dim(power_coef, first_turbine, BLOCK)
            factor = weights[:, None, None] * power_block[None, None, :] * (3.0 / rotor_count)
            adjoint = -factor * velocity ** 4 / speeds[:, None, None]
            adjoint = adjoint.reshape(SPEEDS, rotor_count * BLOCK).astype(jnp.bfloat16)

            def backward(slot_index, back_sum):
                first_source, kernel = tile_for_slot(slot_index)
                back_term = lax.dot_general(adjoint, kernel, (((1,), (1,)), ((), ())), preferred_element_type=jnp.float32)
                current = lax.dynamic_slice_in_dim(back_sum, first_source, BLOCK, 1)
                return lax.dynamic_update_slice_in_dim(back_sum, current + back_term, first_source, 1)

            back_sum = lax.fori_loop(0, in_use, backward, back_sum)
            cube_means = lax.dynamic_update_slice_in_dim(cube_means, cube_mean, first_turbine, 1)
            return cube_means, back_sum

        empty_rows = jnp.zeros((SPEEDS, total_turbines), jnp.float32)
        cube_means, back_sum = lax.fori_loop(0, block_total, one_block, (empty_rows, empty_rows))
        powers.append(power_coef[None, :] * cube_means)
        gradient = gradient + jnp.sum(weights[:, None] * (slope_coef[None, :] * cube_means + thrust_weight[direction] * back_sum), axis=0)
    return jnp.stack(powers), gradient
```

```python
import functools
import math
import jax
import jax.numpy as jnp
from jax import lax
from jax.experimental import pallas as pl
from jax.experimental.pallas import tpu as pltpu
from jax.sharding import PartitionSpec as P

BLOCK = 128
BLKS = 8
GRID = 5
SPEEDS = 16
REACH = 3
PIECES = 2 * REACH + 1
SOURCES = PIECES * BLKS
NULL = SOURCES
PAIRS = 16
ROWS = 16
CHUNKS = BLOCK // ROWS
LANES = 16 * ROWS
LOG2E = math.log2(math.e)
Y_SCALE = math.sqrt(2.0 * LOG2E)
STEP = 0.2 * Y_SCALE
WIDEN = 0.06 / LOG2E


def from_behind(value, axis, by):
    length = lax.axis_size(axis)
    pairs = [(i, i + by) for i in range(length) if 0 <= i + by < length]
    return lax.ppermute(value, axis, pairs)


def wake_tiles(target_x, target_y, source_x, source_y):
    behind = jnp.minimum(source_x - target_x, 0.0)
    ratio = 1.0 / (1.0 - WIDEN * behind)
    q = ratio * ratio
    amp = q - q * jnp.exp2(behind)
    lateral = target_y - source_y
    lateral_q = lateral * q
    centre = amp * jnp.exp2(-(lateral * lateral_q))
    tilt = (2.0 * STEP) * lateral_q
    u1 = jnp.exp2(-(STEP * STEP) * q)
    right = jnp.exp2(-tilt) * u1
    left = jnp.exp2(tilt) * u1
    u2 = u1 * u1
    u4 = u2 * u2
    right1 = centre * right
    left1 = centre * left
    right2 = right1 * (right * u2)
    left2 = left1 * (left * u2)
    base = [left2, left1, centre, right1, right2]
    return base + [k * u1 for k in base] + [k * u4 for k in base]


def farm_kernel(index_ref, pairs_ref, *refs):
    pieces = refs[:PIECES]
    axial_ref, spread_ref, freq_ref = refs[PIECES : PIECES + 3]
    power_ref, direct_ref = refs[PIECES + 3 : PIECES + 5]
    back_refs = refs[PIECES + 5 : 2 * PIECES + 5]
    s_ref, xs_ref, ys_ref, xt_ref, yt_ref, d_ref, a_ref, k_ref, b_ref = refs[2 * PIECES + 5 :]

    for o in range(PIECES):
        for blk in range(BLKS):
            q = o * BLKS + blk
            s_ref[q] = (pieces[o][blk * SPEEDS : (blk + 1) * SPEEDS, :].astype(jnp.bfloat16).astype(jnp.float32) * 0.25).astype(jnp.bfloat16)
            row = SPEEDS * BLKS + blk
            xs_ref[q] = jnp.broadcast_to(pieces[o][row : row + 1, :] * LOG2E, (8, BLOCK))
            row = row + BLKS
            ys_ref[q] = jnp.broadcast_to(pieces[o][row : row + 1, :] * Y_SCALE, (8, BLOCK))
            b_ref[q] = jnp.zeros((SPEEDS, BLOCK), jnp.float32)
    s_ref[NULL] = jnp.zeros((SPEEDS, BLOCK), jnp.bfloat16)
    xs_ref[NULL] = jnp.full((8, BLOCK), 1e6, jnp.float32)
    ys_ref[NULL] = jnp.zeros((8, BLOCK), jnp.float32)
    b_ref[NULL] = jnp.zeros((SPEEDS, BLOCK), jnp.float32)

    freq = freq_ref[...]
    speed = 0.4 + 0.75 * lax.broadcasted_iota(jnp.int32, (SPEEDS, BLOCK), 0).astype(jnp.float32) / (SPEEDS - 1)
    lane = lax.broadcasted_iota(jnp.int32, (SPEEDS, BLOCK), 1)
    low_weight = jnp.where(lane < 5 * ROWS, 1.0, 2.0)
    high_weight = jnp.where(lane < 7 * ROWS, 2.0, 0.0)
    scale = freq * (-0.25 * 3.0 / (GRID * GRID)) / speed

    def one_block(b, carry):
        own = REACH * BLKS + b
        xt_ref[...] = jnp.transpose(jnp.broadcast_to(xs_ref[own][0:1, :], (BLOCK, BLOCK)))
        yt_ref[...] = jnp.transpose(jnp.broadcast_to(ys_ref[own][0:1, :], (BLOCK, BLOCK)))
        d_ref[...] = jnp.zeros_like(d_ref)
        count = pairs_ref[b]

        def forward(p, carry):
            q0 = index_ref[b, 2 * p]
            q1 = index_ref[b, 2 * p + 1]
            strength = jnp.concatenate([s_ref[q0], s_ref[q1]], axis=1)
            sx = [jnp.concatenate([xs_ref[q]] * 2, axis=0) for q in (q0, q1)]
            sy = [jnp.concatenate([ys_ref[q]] * 2, axis=0) for q in (q0, q1)]
            zero = jnp.zeros((ROWS, 2 * BLOCK), jnp.bfloat16)
            for tc in range(CHUNKS):
                tx = xt_ref[tc * ROWS : (tc + 1) * ROWS, :]
                ty = yt_ref[tc * ROWS : (tc + 1) * ROWS, :]
                halves = [wake_tiles(tx, ty, sx[h], sy[h]) for h in range(2)]
                kernel = jnp.concatenate(
                    [jnp.concatenate([k0.astype(jnp.bfloat16), k1.astype(jnp.bfloat16)], axis=1) for k0, k1 in zip(*halves)] + [zero],
                    axis=0,
                )
                k_ref[p, tc * LANES : (tc + 1) * LANES, :] = kernel
                d_ref[tc] += lax.dot_general(strength, kernel, (((1,), (1,)), ((), ())), preferred_element_type=jnp.float32)
            return carry

        lax.fori_loop(0, count, forward, 0)

        cube = jnp.zeros((SPEEDS, BLOCK), jnp.float32)
        for tc in range(CHUNKS):
            coef = spread_ref[b, tc : tc + 1, :] * scale
            v_low = speed / (1.0 + d_ref[tc, :, :BLOCK])
            v_high = speed / (1.0 + d_ref[tc, :, BLOCK:])
            s_low = v_low * v_low
            s_high = v_high * v_high
            a_ref[:, tc * LANES : tc * LANES + BLOCK] = (coef * low_weight * (s_low * s_low)).astype(jnp.bfloat16)
            a_ref[:, tc * LANES + BLOCK : (tc + 1) * LANES] = (coef * high_weight * (s_high * s_high)).astype(jnp.bfloat16)
            total = low_weight * (s_low * v_low) + high_weight * (s_high * v_high)
            total = total + pltpu.roll(total, 64, 1)
            total = total + pltpu.roll(total, 32, 1)
            total = total + pltpu.roll(total, 16, 1)
            cube = jnp.where(lane // ROWS == tc, total, cube)
        cube = cube * (1.0 / (GRID * GRID))
        axial = axial_ref[pl.ds(b, 1), :]
        power_coef = 4.0 * axial * (1.0 - axial) * (1.0 - axial)
        slope_coef = 4.0 * (1.0 - axial) * (1.0 - 3.0 * axial)
        power_ref[:, pl.ds(pl.multiple_of(b * BLOCK, BLOCK), BLOCK)] = power_coef * cube
        direct_ref[pl.ds(b, 1), :] = jnp.sum(freq * (slope_coef * cube), axis=0, keepdims=True)

        def backward(p, carry):
            term = jnp.dot(a_ref[...], k_ref[p], preferred_element_type=jnp.float32)
            b_ref[index_ref[b, 2 * p]] += term[:, :BLOCK]
            b_ref[index_ref[b, 2 * p + 1]] += term[:, BLOCK:]
            return carry

        lax.fori_loop(0, count, backward, 0)
        return carry

    lax.fori_loop(0, BLKS, one_block, 0)
    for o in range(PIECES):
        rows = []
        for blk in range(BLKS):
            strength = pieces[o][blk * SPEEDS : (blk + 1) * SPEEDS, :]
            rows.append(jnp.sum(freq * strength * b_ref[o * BLKS + blk], axis=0, keepdims=True))
        back_refs[o][...] = jnp.concatenate(rows, axis=0)


def farm(index, pairs, pieces, axial, spread, freq):
    f32 = jnp.float32
    smem = pl.BlockSpec(memory_space=pltpu.SMEM)
    vmem = pl.BlockSpec(memory_space=pltpu.VMEM)
    piece = jax.ShapeDtypeStruct((BLKS, BLOCK), f32)
    return pl.pallas_call(
        farm_kernel,
        name="farm",
        out_shape=(jax.ShapeDtypeStruct((SPEEDS, BLKS * BLOCK), f32), piece) + (piece,) * PIECES,
        in_specs=[smem, smem] + [vmem] * (PIECES + 3),
        out_specs=(vmem,) * (PIECES + 2),
        scratch_shapes=[
            pltpu.VMEM((SOURCES + 1, SPEEDS, BLOCK), jnp.bfloat16),
            pltpu.VMEM((SOURCES + 1, 8, BLOCK), f32),
            pltpu.VMEM((SOURCES + 1, 8, BLOCK), f32),
            pltpu.VMEM((BLOCK, BLOCK), f32),
            pltpu.VMEM((BLOCK, BLOCK), f32),
            pltpu.VMEM((CHUNKS, SPEEDS, LANES), f32),
            pltpu.VMEM((SPEEDS, CHUNKS * LANES), jnp.bfloat16),
            pltpu.VMEM((PAIRS // 2, CHUNKS * LANES, 2 * BLOCK), jnp.bfloat16),
            pltpu.VMEM((SOURCES + 1, SPEEDS, BLOCK), f32),
        ],
        compiler_params=pltpu.CompilerParams(vmem_limit_bytes=32 << 20),
        cost_estimate=pl.CostEstimate(flops=2 * 64 * 128 * 2048 * 16 * 2, bytes_accessed=4 << 20, transcendentals=0),
    )(index, pairs, *pieces, axial, spread, freq)


def body(axial, thrust_weight, xdown, ycross, freq, upstream, counts):
    position = lax.axis_index("pt")
    lowest = (position - REACH) * BLKS
    strength = (axial[None, :] * thrust_weight[0]).reshape(SPEEDS, BLKS, BLOCK)
    strength = jnp.transpose(strength, (1, 0, 2)).reshape(BLKS * SPEEDS, BLOCK)
    packed = jnp.concatenate([strength, xdown[0].reshape(BLKS, BLOCK), ycross[0].reshape(BLKS, BLOCK)], axis=0)
    pieces = [packed if o == REACH else from_behind(packed, "pt", REACH - o) for o in range(PIECES)]
    slots = lax.broadcasted_iota(jnp.int32, (BLKS, PAIRS), 1)
    index = jnp.where(slots < counts[0][:, None], upstream[0] - lowest, NULL)
    pairs = (counts[0] + 1) // 2
    axial_rows = axial.reshape(BLKS, BLOCK)
    power_coef = 4.0 * axial_rows * (1.0 - axial_rows) ** 2
    spread = jnp.broadcast_to(power_coef.reshape(BLKS, CHUNKS, 1, ROWS), (BLKS, CHUNKS, BLOCK // ROWS, ROWS)).reshape(BLKS, CHUNKS, BLOCK)
    freq_wide = jnp.broadcast_to(freq[0][:, None], (SPEEDS, BLOCK))
    power, direct, *back = farm(index, pairs, pieces, axial_rows, spread, freq_wide)
    total = back[REACH]
    for o in range(PIECES):
        if o != REACH:
            total = total + from_behind(back[o], "pt", o - REACH)
    gradient = direct + total / axial_rows
    for bit in (1, 2, 4):
        gradient = gradient + lax.ppermute(gradient, "dir", [(i, i ^ bit) for i in range(lax.axis_size("dir"))])
    return power[None], gradient.reshape(-1)


def solution(mesh):
    placed = (
        P("pt"),
        P("dir", None, "pt"),
        P("dir", "pt"),
        P("dir", "pt"),
        P("dir", None),
        P("dir", "pt", None),
        P("dir", "pt"),
    )
    return jax.shard_map(
        body, mesh=mesh, in_specs=placed, out_specs=(P("dir", None, "pt"), P("pt")), check_vma=False
    )
```

```python
import functools
import math
import jax
import jax.numpy as jnp
from jax import lax
from jax.experimental import pallas as pl
from jax.experimental.pallas import tpu as pltpu
from jax.sharding import PartitionSpec as P

BLOCK = 128
BLKS = 8
GRID = 5
SPEEDS = 16
REACH = 3
PIECES = 2 * REACH + 1
GROUP = 8
SOURCES = PIECES * BLKS
NULL = SOURCES
PAIRS = 16
ROWS = 16
CHUNKS = BLOCK // ROWS
LANES = 16 * ROWS
LOG2E = math.log2(math.e)
Y_SCALE = math.sqrt(2.0 * LOG2E)
STEP = 0.2 * Y_SCALE
WIDEN = 0.06 / LOG2E


def from_behind(value, axis, by):
    length = lax.axis_size(axis)
    pairs = [(i, i + by) for i in range(length) if 0 <= i + by < length]
    return lax.ppermute(value, axis, pairs)


def wake_tiles(target_x, target_y, source_x, source_y):
    behind = jnp.minimum(source_x - target_x, 0.0)
    ratio = 1.0 / (1.0 - WIDEN * behind)
    q = ratio * ratio
    amp = q - q * jnp.exp2(behind)
    lateral = target_y - source_y
    lateral_q = lateral * q
    centre = amp * jnp.exp2(-(lateral * lateral_q))
    tilt = (2.0 * STEP) * lateral_q
    u1 = jnp.exp2(-(STEP * STEP) * q)
    right = jnp.exp2(-tilt) * u1
    left = jnp.exp2(tilt) * u1
    u2 = u1 * u1
    u4 = u2 * u2
    right1 = centre * right
    left1 = centre * left
    right2 = right1 * (right * u2)
    left2 = left1 * (left * u2)
    base = [left2, left1, centre, right1, right2]
    return base + [k * u1 for k in base] + [k * u4 for k in base]


def farm_kernel(index_ref, pairs_ref, place_ref, *refs):
    pieces = refs[:PIECES]
    axial_ref, spread_ref, freq_ref = refs[PIECES : PIECES + 3]
    power_ref, direct_ref, send_ref = refs[PIECES + 3 : PIECES + 6]
    s_ref, xs_ref, ys_ref, xt_ref, yt_ref, d_ref, a_ref, k_ref, b_ref, g_ref = refs[PIECES + 6 :]

    for o in range(PIECES):
        for blk in range(BLKS):
            q = o * BLKS + blk
            s_ref[q] = (pieces[o][blk * SPEEDS : (blk + 1) * SPEEDS, :].astype(jnp.bfloat16).astype(jnp.float32) * 0.25).astype(jnp.bfloat16)
            row = SPEEDS * BLKS + blk
            xs_ref[q] = jnp.broadcast_to(pieces[o][row : row + 1, :] * LOG2E, (8, BLOCK))
            row = row + BLKS
            ys_ref[q] = jnp.broadcast_to(pieces[o][row : row + 1, :] * Y_SCALE, (8, BLOCK))
            b_ref[q] = jnp.zeros((SPEEDS, BLOCK), jnp.float32)
    s_ref[NULL] = jnp.zeros((SPEEDS, BLOCK), jnp.bfloat16)
    xs_ref[NULL] = jnp.full((8, BLOCK), 1e6, jnp.float32)
    ys_ref[NULL] = jnp.zeros((8, BLOCK), jnp.float32)
    b_ref[NULL] = jnp.zeros((SPEEDS, BLOCK), jnp.float32)

    freq = freq_ref[...]
    speed = 0.4 + 0.75 * lax.broadcasted_iota(jnp.int32, (SPEEDS, BLOCK), 0).astype(jnp.float32) / (SPEEDS - 1)
    lane = lax.broadcasted_iota(jnp.int32, (SPEEDS, BLOCK), 1)
    low_weight = jnp.where(lane < 5 * ROWS, 1.0, 2.0)
    high_weight = jnp.where(lane < 7 * ROWS, 2.0, 0.0)
    scale = freq * (-0.25 * 3.0 / (GRID * GRID)) / speed

    def one_block(b, carry):
        own = REACH * BLKS + b
        xt_ref[...] = jnp.transpose(jnp.broadcast_to(xs_ref[own][0:1, :], (BLOCK, BLOCK)))
        yt_ref[...] = jnp.transpose(jnp.broadcast_to(ys_ref[own][0:1, :], (BLOCK, BLOCK)))
        d_ref[...] = jnp.zeros_like(d_ref)
        count = pairs_ref[b]

        def forward(p, carry):
            q0 = index_ref[b, 2 * p]
            q1 = index_ref[b, 2 * p + 1]
            strength = jnp.concatenate([s_ref[q0], s_ref[q1]], axis=1)
            sx = [jnp.concatenate([xs_ref[q]] * 2, axis=0) for q in (q0, q1)]
            sy = [jnp.concatenate([ys_ref[q]] * 2, axis=0) for q in (q0, q1)]
            zero = jnp.zeros((ROWS, BLOCK), jnp.bfloat16)
            for tc in range(CHUNKS):
                tx = xt_ref[tc * ROWS : (tc + 1) * ROWS, :]
                ty = yt_ref[tc * ROWS : (tc + 1) * ROWS, :]
                halves = [wake_tiles(tx, ty, sx[h], sy[h]) for h in range(2)]
                columns = [jnp.concatenate([k.astype(jnp.bfloat16) for k in half] + [zero], axis=0) for half in halves]
                for h in range(2):
                    k_ref[p, h, tc * LANES : (tc + 1) * LANES, :] = columns[h]
                kernel = jnp.concatenate(columns, axis=1)
                d_ref[tc] += lax.dot_general(strength, kernel, (((1,), (1,)), ((), ())), preferred_element_type=jnp.float32)
            return carry

        lax.fori_loop(0, count, forward, 0)

        cube = jnp.zeros((SPEEDS, BLOCK), jnp.float32)
        for tc in range(CHUNKS):
            coef = spread_ref[b, tc : tc + 1, :] * scale
            v_low = speed / (1.0 + d_ref[tc, :, :BLOCK])
            v_high = speed / (1.0 + d_ref[tc, :, BLOCK:])
            s_low = v_low * v_low
            s_high = v_high * v_high
            a_ref[:, tc * LANES : tc * LANES + BLOCK] = (coef * low_weight * (s_low * s_low)).astype(jnp.bfloat16)
            a_ref[:, tc * LANES + BLOCK : (tc + 1) * LANES] = (coef * high_weight * (s_high * s_high)).astype(jnp.bfloat16)
            total = low_weight * (s_low * v_low) + high_weight * (s_high * v_high)
            total = total + pltpu.roll(total, 64, 1)
            total = total + pltpu.roll(total, 32, 1)
            total = total + pltpu.roll(total, 16, 1)
            cube = jnp.where(lane // ROWS == tc, total, cube)
        cube = cube * (1.0 / (GRID * GRID))
        axial = axial_ref[pl.ds(b, 1), :]
        power_coef = 4.0 * axial * (1.0 - axial) * (1.0 - axial)
        slope_coef = 4.0 * (1.0 - axial) * (1.0 - 3.0 * axial)
        power_ref[:, pl.ds(pl.multiple_of(b * BLOCK, BLOCK), BLOCK)] = power_coef * cube
        direct_ref[pl.ds(b, 1), :] = jnp.sum(freq * (slope_coef * cube), axis=0, keepdims=True)

        def backward(p, carry):
            kernel = jnp.concatenate([k_ref[p, 0], k_ref[p, 1]], axis=1)
            term = jnp.dot(a_ref[...], kernel, preferred_element_type=jnp.float32)
            b_ref[index_ref[b, 2 * p]] += term[:, :BLOCK]
            b_ref[index_ref[b, 2 * p + 1]] += term[:, BLOCK:]
            return carry

        lax.fori_loop(0, count, backward, 0)
        return carry

    lax.fori_loop(0, BLKS, one_block, 0)
    for o in range(PIECES):
        rows = []
        for blk in range(BLKS):
            strength = pieces[o][blk * SPEEDS : (blk + 1) * SPEEDS, :]
            rows.append(jnp.sum(freq * strength * b_ref[o * BLKS + blk], axis=0, keepdims=True))
        g_ref[GROUP - 1 + o] = jnp.concatenate(rows, axis=0)
    for o in list(range(GROUP - 1)) + list(range(GROUP - 1 + PIECES, 2 * GROUP + PIECES - 2)):
        g_ref[o] = jnp.zeros((BLKS, BLOCK), jnp.float32)
    place = place_ref[0]
    for i in range(GROUP):
        first = i - place + GROUP - 1
        send_ref[i, 0] = g_ref[first + REACH]
        if i < REACH:
            send_ref[i, 1] = g_ref[first]
        elif i >= GROUP - REACH:
            send_ref[i, 1] = g_ref[first + 2 * REACH]
        else:
            send_ref[i, 1] = jnp.zeros((BLKS, BLOCK), jnp.float32)


def farm(index, pairs, place, pieces, axial, spread, freq):
    f32 = jnp.float32
    smem = pl.BlockSpec(memory_space=pltpu.SMEM)
    vmem = pl.BlockSpec(memory_space=pltpu.VMEM)
    piece = jax.ShapeDtypeStruct((BLKS, BLOCK), f32)
    return pl.pallas_call(
        farm_kernel,
        name="farm",
        out_shape=(jax.ShapeDtypeStruct((SPEEDS, BLKS * BLOCK), f32), piece, jax.ShapeDtypeStruct((GROUP, 2, BLKS, BLOCK), f32)),
        in_specs=[smem, smem, smem] + [vmem] * (PIECES + 3),
        out_specs=(vmem,) * 3,
        scratch_shapes=[
            pltpu.VMEM((SOURCES + 1, SPEEDS, BLOCK), jnp.bfloat16),
            pltpu.VMEM((SOURCES + 1, 8, BLOCK), f32),
            pltpu.VMEM((SOURCES + 1, 8, BLOCK), f32),
            pltpu.VMEM((BLOCK, BLOCK), f32),
            pltpu.VMEM((BLOCK, BLOCK), f32),
            pltpu.VMEM((CHUNKS, SPEEDS, LANES), f32),
            pltpu.VMEM((SPEEDS, CHUNKS * LANES), jnp.bfloat16),
            pltpu.VMEM((PAIRS // 2, 2, CHUNKS * LANES, BLOCK), jnp.bfloat16),
            pltpu.VMEM((SOURCES + 1, SPEEDS, BLOCK), f32),
            pltpu.VMEM((2 * GROUP + PIECES - 2, BLKS, BLOCK), f32),
        ],
        compiler_params=pltpu.CompilerParams(vmem_limit_bytes=32 << 20),
        cost_estimate=pl.CostEstimate(flops=2 * 64 * 128 * 2048 * 16 * 2, bytes_accessed=4 << 20, transcendentals=0),
    )(index, pairs, place, *pieces, axial, spread, freq)


def body(axial, thrust_weight, xdown, ycross, freq, upstream, counts):
    position = lax.axis_index("pt")
    lowest = (position - REACH) * BLKS
    strength = (axial[None, :] * thrust_weight[0]).reshape(SPEEDS, BLKS, BLOCK)
    strength = jnp.transpose(strength, (1, 0, 2)).reshape(BLKS * SPEEDS, BLOCK)
    packed = jnp.concatenate([strength, xdown[0].reshape(BLKS, BLOCK), ycross[0].reshape(BLKS, BLOCK)], axis=0)
    pieces = [packed if o == REACH else from_behind(packed, "pt", REACH - o) for o in range(PIECES)]
    slots = lax.broadcasted_iota(jnp.int32, (BLKS, PAIRS), 1)
    index = jnp.where(slots < counts[0][:, None], upstream[0] - lowest, NULL)
    pairs = (counts[0] + 1) // 2
    axial_rows = axial.reshape(BLKS, BLOCK)
    power_coef = 4.0 * axial_rows * (1.0 - axial_rows) ** 2
    spread = jnp.broadcast_to(power_coef.reshape(BLKS, CHUNKS, 1, ROWS), (BLKS, CHUNKS, BLOCK // ROWS, ROWS)).reshape(BLKS, CHUNKS, BLOCK)
    freq_wide = jnp.broadcast_to(freq[0][:, None], (SPEEDS, BLOCK))
    place = (position % GROUP).reshape(1)
    power, direct, send = farm(index, pairs, place, pieces, axial_rows, spread, freq_wide)
    length = lax.axis_size("pt")
    groups = [list(range(a, a + GROUP)) for a in range(0, length, GROUP)]
    arrived = jnp.sum(lax.all_to_all(send, "pt", 0, 0, axis_index_groups=groups), axis=0)
    across = []
    for a in range(GROUP, length, GROUP):
        for i in range(REACH):
            across += [(a - REACH + i, a + i), (a + i, a - REACH + i)]
    total = arrived[0] + lax.ppermute(arrived[1], "pt", across)
    gradient = direct + total / axial_rows
    spread_out = jnp.broadcast_to(gradient[None], (lax.axis_size("dir"),) + gradient.shape)
    gradient = jnp.sum(lax.all_to_all(spread_out, "dir", 0, 0), axis=0)
    return power[None], gradient.reshape(-1)


def solution(mesh):
    placed = (
        P("pt"),
        P("dir", None, "pt"),
        P("dir", "pt"),
        P("dir", "pt"),
        P("dir", None),
        P("dir", "pt", None),
        P("dir", "pt"),
    )
    return jax.shard_map(
        body, mesh=mesh, in_specs=placed, out_specs=(P("dir", None, "pt"), P("pt")), check_vma=False
    )
```

```python
import functools
import math
import jax
import jax.numpy as jnp
from jax import lax
from jax.experimental import pallas as pl
from jax.experimental.pallas import tpu as pltpu
from jax.sharding import PartitionSpec as P

BLOCK = 128
BLKS = 8
GRID = 5
SPEEDS = 16
REACH = 3
PIECES = 2 * REACH + 1
GROUP = 8
SOURCES = PIECES * BLKS
NULL = SOURCES
PAIRS = 16
ROWS = 16
CHUNKS = BLOCK // ROWS
LANES = 16 * ROWS
LOG2E = math.log2(math.e)
Y_SCALE = math.sqrt(2.0 * LOG2E)
STEP = 0.2 * Y_SCALE
WIDEN = 0.06 / LOG2E


def wake_tiles(target_x, target_y, source_x, source_y):
    behind = jnp.minimum(source_x - target_x, 0.0)
    ratio = 1.0 / (1.0 - WIDEN * behind)
    q = ratio * ratio
    amp = q - q * jnp.exp2(behind)
    lateral = target_y - source_y
    lateral_q = lateral * q
    centre = amp * jnp.exp2(-(lateral * lateral_q))
    tilt = (2.0 * STEP) * lateral_q
    u1 = jnp.exp2(-(STEP * STEP) * q)
    right = jnp.exp2(-tilt) * u1
    left = jnp.exp2(tilt) * u1
    u2 = u1 * u1
    u4 = u2 * u2
    right1 = centre * right
    left1 = centre * left
    right2 = right1 * (right * u2)
    left2 = left1 * (left * u2)
    base = [left2, left1, centre, right1, right2]
    return base + [k * u1 for k in base] + [k * u4 for k in base]


def farm_kernel(index_ref, pairs_ref, place_ref, *refs):
    pieces = refs[:PIECES]
    axial_ref, spread_ref, freq_ref = refs[PIECES : PIECES + 3]
    power_ref, direct_ref, send_ref = refs[PIECES + 3 : PIECES + 6]
    s_ref, xs_ref, ys_ref, xt_ref, yt_ref, d_ref, a_ref, k_ref, b_ref, g_ref = refs[PIECES + 6 :]

    for o in range(PIECES):
        for blk in range(BLKS):
            q = o * BLKS + blk
            s_ref[q] = (pieces[o][blk * SPEEDS : (blk + 1) * SPEEDS, :].astype(jnp.bfloat16).astype(jnp.float32) * 0.25).astype(jnp.bfloat16)
            row = SPEEDS * BLKS + blk
            xs_ref[q] = jnp.broadcast_to(pieces[o][row : row + 1, :] * LOG2E, (8, BLOCK))
            row = row + BLKS
            ys_ref[q] = jnp.broadcast_to(pieces[o][row : row + 1, :] * Y_SCALE, (8, BLOCK))
            b_ref[q] = jnp.zeros((SPEEDS, BLOCK), jnp.float32)
    s_ref[NULL] = jnp.zeros((SPEEDS, BLOCK), jnp.bfloat16)
    xs_ref[NULL] = jnp.full((8, BLOCK), 1e6, jnp.float32)
    ys_ref[NULL] = jnp.zeros((8, BLOCK), jnp.float32)
    b_ref[NULL] = jnp.zeros((SPEEDS, BLOCK), jnp.float32)

    freq = freq_ref[...]
    speed = 0.4 + 0.75 * lax.broadcasted_iota(jnp.int32, (SPEEDS, BLOCK), 0).astype(jnp.float32) / (SPEEDS - 1)
    lane = lax.broadcasted_iota(jnp.int32, (SPEEDS, BLOCK), 1)
    low_weight = jnp.where(lane < 5 * ROWS, 1.0, 2.0)
    high_weight = jnp.where(lane < 7 * ROWS, 2.0, 0.0)
    scale = freq * (-0.25 * 3.0 / (GRID * GRID)) / speed

    def one_block(b, carry):
        own = REACH * BLKS + b
        xt_ref[...] = jnp.transpose(jnp.broadcast_to(xs_ref[own][0:1, :], (BLOCK, BLOCK)))
        yt_ref[...] = jnp.transpose(jnp.broadcast_to(ys_ref[own][0:1, :], (BLOCK, BLOCK)))
        d_ref[...] = jnp.zeros_like(d_ref)
        count = pairs_ref[b]

        def forward(p, carry):
            q0 = index_ref[b, 2 * p]
            q1 = index_ref[b, 2 * p + 1]
            strength = jnp.concatenate([s_ref[q0], s_ref[q1]], axis=1)
            sx = [jnp.concatenate([xs_ref[q]] * 2, axis=0) for q in (q0, q1)]
            sy = [jnp.concatenate([ys_ref[q]] * 2, axis=0) for q in (q0, q1)]
            zero = jnp.zeros((ROWS, BLOCK), jnp.bfloat16)
            for tc in range(CHUNKS):
                tx = xt_ref[tc * ROWS : (tc + 1) * ROWS, :]
                ty = yt_ref[tc * ROWS : (tc + 1) * ROWS, :]
                halves = [wake_tiles(tx, ty, sx[h], sy[h]) for h in range(2)]
                columns = [jnp.concatenate([k.astype(jnp.bfloat16) for k in half] + [zero], axis=0) for half in halves]
                for h in range(2):
                    k_ref[p, h, tc * LANES : (tc + 1) * LANES, :] = columns[h]
                kernel = jnp.concatenate(columns, axis=1)
                d_ref[tc] += lax.dot_general(strength, kernel, (((1,), (1,)), ((), ())), preferred_element_type=jnp.float32)
            return carry

        lax.fori_loop(0, count, forward, 0)

        cube = jnp.zeros((SPEEDS, BLOCK), jnp.float32)
        for tc in range(CHUNKS):
            coef = spread_ref[b, tc : tc + 1, :] * scale
            v_low = speed / (1.0 + d_ref[tc, :, :BLOCK])
            v_high = speed / (1.0 + d_ref[tc, :, BLOCK:])
            s_low = v_low * v_low
            s_high = v_high * v_high
            a_ref[:, tc * LANES : tc * LANES + BLOCK] = (coef * low_weight * (s_low * s_low)).astype(jnp.bfloat16)
            a_ref[:, tc * LANES + BLOCK : (tc + 1) * LANES] = (coef * high_weight * (s_high * s_high)).astype(jnp.bfloat16)
            total = low_weight * (s_low * v_low) + high_weight * (s_high * v_high)
            total = total + pltpu.roll(total, 64, 1)
            total = total + pltpu.roll(total, 32, 1)
            total = total + pltpu.roll(total, 16, 1)
            cube = jnp.where(lane // ROWS == tc, total, cube)
        cube = cube * (1.0 / (GRID * GRID))
        axial = axial_ref[pl.ds(b, 1), :]
        power_coef = 4.0 * axial * (1.0 - axial) * (1.0 - axial)
        slope_coef = 4.0 * (1.0 - axial) * (1.0 - 3.0 * axial)
        power_ref[:, pl.ds(pl.multiple_of(b * BLOCK, BLOCK), BLOCK)] = power_coef * cube
        direct_ref[pl.ds(b, 1), :] = jnp.sum(freq * (slope_coef * cube), axis=0, keepdims=True)

        def backward(p, carry):
            kernel = jnp.concatenate([k_ref[p, 0], k_ref[p, 1]], axis=1)
            term = jnp.dot(a_ref[...], kernel, preferred_element_type=jnp.float32)
            b_ref[index_ref[b, 2 * p]] += term[:, :BLOCK]
            b_ref[index_ref[b, 2 * p + 1]] += term[:, BLOCK:]
            return carry

        lax.fori_loop(0, count, backward, 0)
        return carry

    lax.fori_loop(0, BLKS, one_block, 0)
    for o in range(PIECES):
        rows = []
        for blk in range(BLKS):
            strength = pieces[o][blk * SPEEDS : (blk + 1) * SPEEDS, :]
            rows.append(jnp.sum(freq * strength * b_ref[o * BLKS + blk], axis=0, keepdims=True))
        g_ref[GROUP - 1 + jnp.where(place_ref[1] == 0, o, PIECES - 1 - o)] = jnp.concatenate(rows, axis=0)
    for o in list(range(GROUP - 1)) + list(range(GROUP - 1 + PIECES, 2 * GROUP + PIECES - 2)):
        g_ref[o] = jnp.zeros((BLKS, BLOCK), jnp.float32)
    place = place_ref[0]
    for i in range(GROUP):
        first = i - place + GROUP - 1
        send_ref[i, 0] = g_ref[first + REACH]
        if i < REACH:
            send_ref[i, 1] = g_ref[first]
        elif i >= GROUP - REACH:
            send_ref[i, 1] = g_ref[first + 2 * REACH]
        else:
            send_ref[i, 1] = jnp.zeros((BLKS, BLOCK), jnp.float32)


def farm(index, pairs, place, pieces, axial, spread, freq):
    f32 = jnp.float32
    smem = pl.BlockSpec(memory_space=pltpu.SMEM)
    vmem = pl.BlockSpec(memory_space=pltpu.VMEM)
    piece = jax.ShapeDtypeStruct((BLKS, BLOCK), f32)
    return pl.pallas_call(
        farm_kernel,
        name="farm",
        out_shape=(jax.ShapeDtypeStruct((SPEEDS, BLKS * BLOCK), f32), piece, jax.ShapeDtypeStruct((GROUP, 2, BLKS, BLOCK), f32)),
        in_specs=[smem, smem, smem] + [vmem] * (PIECES + 3),
        out_specs=(vmem,) * 3,
        scratch_shapes=[
            pltpu.VMEM((SOURCES + 1, SPEEDS, BLOCK), jnp.bfloat16),
            pltpu.VMEM((SOURCES + 1, 8, BLOCK), f32),
            pltpu.VMEM((SOURCES + 1, 8, BLOCK), f32),
            pltpu.VMEM((BLOCK, BLOCK), f32),
            pltpu.VMEM((BLOCK, BLOCK), f32),
            pltpu.VMEM((CHUNKS, SPEEDS, LANES), f32),
            pltpu.VMEM((SPEEDS, CHUNKS * LANES), jnp.bfloat16),
            pltpu.VMEM((PAIRS // 2, 2, CHUNKS * LANES, BLOCK), jnp.bfloat16),
            pltpu.VMEM((SOURCES + 1, SPEEDS, BLOCK), f32),
            pltpu.VMEM((2 * GROUP + PIECES - 2, BLKS, BLOCK), f32),
        ],
        compiler_params=pltpu.CompilerParams(vmem_limit_bytes=32 << 20),
        cost_estimate=pl.CostEstimate(flops=2 * 64 * 128 * 2048 * 16 * 2, bytes_accessed=4 << 20, transcendentals=0),
    )(index, pairs, place, *pieces, axial, spread, freq)


def body(axial, thrust_weight, xdown, ycross, freq, upstream, counts):
    position = lax.axis_index("pt")
    lowest = (position - REACH) * BLKS
    strength = (axial[None, :] * thrust_weight[0]).reshape(SPEEDS, BLKS, BLOCK)
    strength = jnp.transpose(strength, (1, 0, 2)).reshape(BLKS * SPEEDS, BLOCK)
    packed = jnp.concatenate([strength, xdown[0].reshape(BLKS, BLOCK), ycross[0].reshape(BLKS, BLOCK)], axis=0)
    length = lax.axis_size("pt")
    core = position % 2
    swap = [(i, i ^ 1) for i in range(length)]
    hops = [[(i, i + by if i % 2 == up else i - by) for i in range(length)] for by, up in ((1, 1), (2, 0), (3, 1))]
    hops = [[(i, j) for i, j in pairs if 0 <= j < length] for pairs in hops]
    near, middle, far = [lax.ppermute(packed, "pt", pairs) for pairs in hops]
    turned = [lax.ppermute(value, "pt", swap) for value in (packed, near, middle)]
    pieces = [far, middle, near, packed] + turned
    slots = lax.broadcasted_iota(jnp.int32, (BLKS, PAIRS), 1)
    local = upstream[0] - lowest
    local = jnp.where(core == 0, local, (PIECES - 1) * BLKS - local + 2 * (local % BLKS))
    index = jnp.where(slots < counts[0][:, None], local, NULL)
    pairs = (counts[0] + 1) // 2
    axial_rows = axial.reshape(BLKS, BLOCK)
    power_coef = 4.0 * axial_rows * (1.0 - axial_rows) ** 2
    spread = jnp.broadcast_to(power_coef.reshape(BLKS, CHUNKS, 1, ROWS), (BLKS, CHUNKS, BLOCK // ROWS, ROWS)).reshape(BLKS, CHUNKS, BLOCK)
    freq_wide = jnp.broadcast_to(freq[0][:, None], (SPEEDS, BLOCK))
    place = jnp.stack([position % GROUP, core])
    power, direct, send = farm(index, pairs, place, pieces, axial_rows, spread, freq_wide)
    groups = [list(range(a, a + GROUP)) for a in range(0, length, GROUP)]
    arrived = jnp.sum(lax.all_to_all(send, "pt", 0, 0, axis_index_groups=groups), axis=0)
    across = []
    for a in range(GROUP, length, GROUP):
        for i in range(REACH):
            across += [(a - REACH + i, a + i), (a + i, a - REACH + i)]
    total = arrived[0] + lax.ppermute(arrived[1], "pt", across)
    gradient = direct + total / axial_rows
    spread_out = jnp.broadcast_to(gradient[None], (lax.axis_size("dir"),) + gradient.shape)
    gradient = jnp.sum(lax.all_to_all(spread_out, "dir", 0, 0), axis=0)
    return power[None], gradient.reshape(-1)


def solution(mesh):
    placed = (
        P("pt"),
        P("dir", None, "pt"),
        P("dir", "pt"),
        P("dir", "pt"),
        P("dir", None),
        P("dir", "pt", None),
        P("dir", "pt"),
    )
    return jax.shard_map(
        body, mesh=mesh, in_specs=placed, out_specs=(P("dir", None, "pt"), P("pt")), check_vma=False
    )
```

```python
import functools
import math
import jax
import jax.numpy as jnp
from jax import lax
from jax.experimental import pallas as pl
from jax.experimental.pallas import tpu as pltpu
from jax.sharding import PartitionSpec as P

BLOCK = 128
BLKS = 8
GRID = 5
SPEEDS = 16
REACH = 3
PIECES = 2 * REACH + 1
GROUP = 8
SOURCES = PIECES * BLKS
NULL = SOURCES
PAIRS = 16
ROWS = 16
CHUNKS = BLOCK // ROWS
LANES = 16 * ROWS
LOG2E = math.log2(math.e)
Y_SCALE = math.sqrt(2.0 * LOG2E)
STEP = 0.2 * Y_SCALE
WIDEN = 0.06 / LOG2E


def wake_tiles(target_x, target_y, source_x, source_y):
    behind = jnp.minimum(source_x - target_x, 0.0)
    ratio = 1.0 / (1.0 - WIDEN * behind)
    q = ratio * ratio
    amp = q - q * jnp.exp2(behind)
    lateral = target_y - source_y
    lateral_q = lateral * q
    centre = amp * jnp.exp2(-(lateral * lateral_q))
    tilt = (2.0 * STEP) * lateral_q
    u1 = jnp.exp2(-(STEP * STEP) * q)
    right = jnp.exp2(-tilt) * u1
    left = jnp.exp2(tilt) * u1
    u2 = u1 * u1
    u4 = u2 * u2
    right1 = centre * right
    left1 = centre * left
    right2 = right1 * (right * u2)
    left2 = left1 * (left * u2)
    base = [left2, left1, centre, right1, right2]
    return base + [k * u1 for k in base] + [k * u4 for k in base]


def farm_kernel(index_ref, pairs_ref, place_ref, *refs):
    pieces = refs[:PIECES]
    axial_ref, spread_ref, freq_ref = refs[PIECES : PIECES + 3]
    power_ref, direct_ref, send_ref = refs[PIECES + 3 : PIECES + 6]
    s_ref, xs_ref, ys_ref, xt_ref, yt_ref, d_ref, a_ref, k_ref, b_ref, g_ref = refs[PIECES + 6 :]

    for o in range(PIECES):
        for blk in range(BLKS):
            q = o * BLKS + blk
            s_ref[q] = (pieces[o][blk * SPEEDS : (blk + 1) * SPEEDS, :] * 0.25).astype(jnp.bfloat16)
            row = SPEEDS * BLKS + blk
            xs_ref[q] = jnp.broadcast_to(pieces[o][row : row + 1, :] * LOG2E, (8, BLOCK))
            row = row + BLKS
            ys_ref[q] = jnp.broadcast_to(pieces[o][row : row + 1, :] * Y_SCALE, (8, BLOCK))
            b_ref[q] = jnp.zeros((SPEEDS, BLOCK), jnp.float32)
    s_ref[NULL] = jnp.zeros((SPEEDS, BLOCK), jnp.bfloat16)
    xs_ref[NULL] = jnp.full((8, BLOCK), 1e6, jnp.float32)
    ys_ref[NULL] = jnp.zeros((8, BLOCK), jnp.float32)
    b_ref[NULL] = jnp.zeros((SPEEDS, BLOCK), jnp.float32)

    freq = freq_ref[...]
    speed = 0.4 + 0.75 * lax.broadcasted_iota(jnp.int32, (SPEEDS, BLOCK), 0).astype(jnp.float32) / (SPEEDS - 1)
    lane = lax.broadcasted_iota(jnp.int32, (SPEEDS, BLOCK), 1)
    low_weight = jnp.where(lane < 5 * ROWS, 1.0, 2.0)
    high_weight = jnp.where(lane < 7 * ROWS, 2.0, 0.0)
    scale = freq * (-0.25 * 3.0 / (GRID * GRID)) / speed

    def one_block(b, carry):
        own = REACH * BLKS + b
        xt_ref[...] = jnp.transpose(jnp.broadcast_to(xs_ref[own][0:1, :], (BLOCK, BLOCK)))
        yt_ref[...] = jnp.transpose(jnp.broadcast_to(ys_ref[own][0:1, :], (BLOCK, BLOCK)))
        d_ref[...] = jnp.zeros_like(d_ref)
        count = pairs_ref[b]

        def forward(p, carry):
            q0 = index_ref[b, 2 * p]
            q1 = index_ref[b, 2 * p + 1]
            strength = jnp.concatenate([s_ref[q0], s_ref[q1]], axis=1)
            sx = [jnp.concatenate([xs_ref[q]] * 2, axis=0) for q in (q0, q1)]
            sy = [jnp.concatenate([ys_ref[q]] * 2, axis=0) for q in (q0, q1)]
            zero = jnp.zeros((ROWS, BLOCK), jnp.bfloat16)
            for tc in range(CHUNKS):
                tx = xt_ref[tc * ROWS : (tc + 1) * ROWS, :]
                ty = yt_ref[tc * ROWS : (tc + 1) * ROWS, :]
                halves = [wake_tiles(tx, ty, sx[h], sy[h]) for h in range(2)]
                columns = [jnp.concatenate([k.astype(jnp.bfloat16) for k in half] + [zero], axis=0) for half in halves]
                for h in range(2):
                    k_ref[p, h, tc * LANES : (tc + 1) * LANES, :] = columns[h]
                if tc in (2, 5):
                    kernel = jnp.concatenate([jnp.transpose(column) for column in columns], axis=0)
                    d_ref[tc] += jnp.dot(strength, kernel, preferred_element_type=jnp.float32)
                else:
                    kernel = jnp.concatenate(columns, axis=1)
                    d_ref[tc] += lax.dot_general(strength, kernel, (((1,), (1,)), ((), ())), preferred_element_type=jnp.float32)
            return carry

        lax.fori_loop(0, count, forward, 0)

        sums = []
        for tc in range(CHUNKS):
            coef = spread_ref[b, tc : tc + 1, :] * scale
            v_low = speed / (1.0 + d_ref[tc, :, :BLOCK])
            v_high = speed / (1.0 + d_ref[tc, :, BLOCK:])
            s_low = v_low * v_low
            s_high = v_high * v_high
            a_ref[:, tc * LANES : tc * LANES + BLOCK] = (coef * low_weight * (s_low * s_low)).astype(jnp.bfloat16)
            a_ref[:, tc * LANES + BLOCK : (tc + 1) * LANES] = (coef * high_weight * (s_high * s_high)).astype(jnp.bfloat16)
            total = low_weight * (s_low * v_low) + high_weight * (s_high * v_high)
            sums.append(total)
        for shift in (64, 32, 16):
            upper = (lane & shift) != 0
            half = len(sums) // 2
            merged = []
            for low, high in zip(sums[:half], sums[half:]):
                other = jnp.where(upper, low, high)
                moved = pltpu.roll(other, shift, 1)
                if shift != 64:
                    moved = jnp.where(upper, moved, pltpu.roll(other, BLOCK - shift, 1))
                merged.append(jnp.where(upper, high, low) + moved)
            sums = merged
        cube = sums[0] * (1.0 / (GRID * GRID))
        axial = axial_ref[pl.ds(b, 1), :]
        power_coef = 4.0 * axial * (1.0 - axial) * (1.0 - axial)
        slope_coef = 4.0 * (1.0 - axial) * (1.0 - 3.0 * axial)
        power_ref[:, pl.ds(pl.multiple_of(b * BLOCK, BLOCK), BLOCK)] = power_coef * cube
        direct_ref[pl.ds(b, 1), :] = jnp.sum(freq * (slope_coef * cube), axis=0, keepdims=True)

        def backward(p, carry):
            kernel = jnp.concatenate([k_ref[p, 0], k_ref[p, 1]], axis=1)
            term = jnp.dot(a_ref[...], kernel, preferred_element_type=jnp.float32)
            b_ref[index_ref[b, 2 * p]] += term[:, :BLOCK]
            b_ref[index_ref[b, 2 * p + 1]] += term[:, BLOCK:]
            return carry

        lax.fori_loop(0, count, backward, 0)
        return carry

    lax.fori_loop(0, BLKS, one_block, 0)
    for o in range(PIECES):
        rows = []
        for blk in range(BLKS):
            strength = pieces[o][blk * SPEEDS : (blk + 1) * SPEEDS, :]
            rows.append(jnp.sum(freq * strength * b_ref[o * BLKS + blk], axis=0, keepdims=True))
        g_ref[GROUP - 1 + jnp.where(place_ref[1] == 0, o, PIECES - 1 - o)] = jnp.concatenate(rows, axis=0)
    for o in list(range(GROUP - 1)) + list(range(GROUP - 1 + PIECES, 2 * GROUP + PIECES - 2)):
        g_ref[o] = jnp.zeros((BLKS, BLOCK), jnp.float32)
    place = place_ref[0]
    for i in range(GROUP):
        first = i - place + GROUP - 1
        send_ref[i, 0] = g_ref[first + REACH]
        if i < REACH:
            send_ref[i, 1] = g_ref[first]
        elif i >= GROUP - REACH:
            send_ref[i, 1] = g_ref[first + 2 * REACH]
        else:
            send_ref[i, 1] = jnp.zeros((BLKS, BLOCK), jnp.float32)


def farm(index, pairs, place, pieces, axial, spread, freq):
    f32 = jnp.float32
    smem = pl.BlockSpec(memory_space=pltpu.SMEM)
    vmem = pl.BlockSpec(memory_space=pltpu.VMEM)
    piece = jax.ShapeDtypeStruct((BLKS, BLOCK), f32)
    return pl.pallas_call(
        farm_kernel,
        name="farm",
        out_shape=(jax.ShapeDtypeStruct((SPEEDS, BLKS * BLOCK), f32), piece, jax.ShapeDtypeStruct((GROUP, 2, BLKS, BLOCK), f32)),
        in_specs=[smem, smem, smem] + [vmem] * (PIECES + 3),
        out_specs=(vmem,) * 3,
        scratch_shapes=[
            pltpu.VMEM((SOURCES + 1, SPEEDS, BLOCK), jnp.bfloat16),
            pltpu.VMEM((SOURCES + 1, 8, BLOCK), f32),
            pltpu.VMEM((SOURCES + 1, 8, BLOCK), f32),
            pltpu.VMEM((BLOCK, BLOCK), f32),
            pltpu.VMEM((BLOCK, BLOCK), f32),
            pltpu.VMEM((CHUNKS, SPEEDS, LANES), f32),
            pltpu.VMEM((SPEEDS, CHUNKS * LANES), jnp.bfloat16),
            pltpu.VMEM((PAIRS // 2, 2, CHUNKS * LANES, BLOCK), jnp.bfloat16),
            pltpu.VMEM((SOURCES + 1, SPEEDS, BLOCK), f32),
            pltpu.VMEM((2 * GROUP + PIECES - 2, BLKS, BLOCK), f32),
        ],
        compiler_params=pltpu.CompilerParams(vmem_limit_bytes=32 << 20),
        cost_estimate=pl.CostEstimate(flops=2 * 64 * 128 * 2048 * 16 * 2, bytes_accessed=4 << 20, transcendentals=0),
    )(index, pairs, place, *pieces, axial, spread, freq)


def body(axial, thrust_weight, xdown, ycross, freq, upstream, counts):
    position = lax.axis_index("pt")
    lowest = (position - REACH) * BLKS
    strength = (axial[None, :] * thrust_weight[0]).reshape(SPEEDS, BLKS, BLOCK)
    strength = jnp.transpose(strength, (1, 0, 2)).reshape(BLKS * SPEEDS, BLOCK)
    packed = jnp.concatenate([strength, xdown[0].reshape(BLKS, BLOCK), ycross[0].reshape(BLKS, BLOCK)], axis=0)
    length = lax.axis_size("pt")
    core = position % 2
    swap = [(i, i ^ 1) for i in range(length)]
    hops = [[(i, i + by if i % 2 == up else i - by) for i in range(length)] for by, up in ((1, 1), (2, 0), (3, 1))]
    hops = [[(i, j) for i, j in pairs if 0 <= j < length] for pairs in hops]
    near, middle, far = [lax.ppermute(packed, "pt", pairs) for pairs in hops]
    turned = [lax.ppermute(value, "pt", swap) for value in (packed, near, middle)]
    pieces = [far, middle, near, packed] + turned
    slots = lax.broadcasted_iota(jnp.int32, (BLKS, PAIRS), 1)
    local = upstream[0] - lowest
    local = jnp.where(core == 0, local, (PIECES - 1) * BLKS - local + 2 * (local % BLKS))
    index = jnp.where(slots < counts[0][:, None], local, NULL)
    pairs = (counts[0] + 1) // 2
    axial_rows = axial.reshape(BLKS, BLOCK)
    power_coef = 4.0 * axial_rows * (1.0 - axial_rows) ** 2
    spread = jnp.broadcast_to(power_coef.reshape(BLKS, CHUNKS, 1, ROWS), (BLKS, CHUNKS, BLOCK // ROWS, ROWS)).reshape(BLKS, CHUNKS, BLOCK)
    freq_wide = jnp.broadcast_to(freq[0][:, None], (SPEEDS, BLOCK))
    place = jnp.stack([position % GROUP, core])
    power, direct, send = farm(index, pairs, place, pieces, axial_rows, spread, freq_wide)
    groups = [list(range(a, a + GROUP)) for a in range(0, length, GROUP)]
    arrived = jnp.sum(lax.all_to_all(send, "pt", 0, 0, axis_index_groups=groups), axis=0)
    across = []
    for a in range(GROUP, length, GROUP):
        for i in range(REACH):
            across += [(a - REACH + i, a + i), (a + i, a - REACH + i)]
    total = arrived[0] + lax.ppermute(arrived[1], "pt", across)
    gradient = direct + total / axial_rows
    spread_out = jnp.broadcast_to(gradient[None], (lax.axis_size("dir"),) + gradient.shape)
    gradient = jnp.sum(lax.all_to_all(spread_out, "dir", 0, 0), axis=0)
    return power[None], gradient.reshape(-1)


def solution(mesh):
    placed = (
        P("pt"),
        P("dir", None, "pt"),
        P("dir", "pt"),
        P("dir", "pt"),
        P("dir", None),
        P("dir", "pt", None),
        P("dir", "pt"),
    )
    return jax.shard_map(
        body, mesh=mesh, in_specs=placed, out_specs=(P("dir", None, "pt"), P("pt")), check_vma=False
    )
```

```python
import functools
import math
import jax
import jax.numpy as jnp
from jax import lax
from jax.experimental import pallas as pl
from jax.experimental.pallas import tpu as pltpu
from jax.sharding import PartitionSpec as P

BLOCK = 128
BLKS = 8
GRID = 5
SPEEDS = 16
REACH = 3
PIECES = 2 * REACH + 1
GROUP = 8
SOURCES = PIECES * BLKS
NULL = SOURCES
PAIRS = 16
LAG = 9
RING = 8
ROWS = 16
CHUNKS = BLOCK // ROWS
LANES = 16 * ROWS
LOG2E = math.log2(math.e)
Y_SCALE = math.sqrt(2.0 * LOG2E)
STEP = 0.2 * Y_SCALE
WIDEN = 0.06 / LOG2E


def wake_tiles(target_x, target_y, source_x, source_y):
    behind = jnp.minimum(source_x - target_x, 0.0)
    ratio = 1.0 / (1.0 - WIDEN * behind)
    q = ratio * ratio
    amp = q - q * jnp.exp2(behind)
    lateral = target_y - source_y
    lateral_q = lateral * q
    centre = amp * jnp.exp2(-(lateral * lateral_q))
    tilt = (2.0 * STEP) * lateral_q
    u1 = jnp.exp2(-(STEP * STEP) * q)
    right = jnp.exp2(-tilt) * u1
    left = jnp.exp2(tilt) * u1
    u2 = u1 * u1
    u4 = u2 * u2
    right1 = centre * right
    left1 = centre * left
    right2 = right1 * (right * u2)
    left2 = left1 * (left * u2)
    base = [left2, left1, centre, right1, right2]
    return base + [k * u1 for k in base] + [k * u4 for k in base]


def farm_kernel(index_ref, pairs_ref, place_ref, *refs):
    pieces = refs[:PIECES]
    axial_ref, spread_ref, freq_ref = refs[PIECES : PIECES + 3]
    power_ref, direct_ref, send_ref = refs[PIECES + 3 : PIECES + 6]
    s_ref, xs_ref, ys_ref, xt_ref, yt_ref, d_ref, a_ref, k0_ref, k1_ref, b_ref, g_ref, note_ref = refs[PIECES + 6 :]

    for o in range(PIECES):
        for blk in range(BLKS):
            q = o * BLKS + blk
            s_ref[q] = (pieces[o][blk * SPEEDS : (blk + 1) * SPEEDS, :] * 0.25).astype(jnp.bfloat16)
            row = SPEEDS * BLKS + blk
            xs_ref[q] = jnp.broadcast_to(pieces[o][row : row + 1, :] * LOG2E, (8, BLOCK))
            row = row + BLKS
            ys_ref[q] = jnp.broadcast_to(pieces[o][row : row + 1, :] * Y_SCALE, (8, BLOCK))
            b_ref[q] = jnp.zeros((SPEEDS, BLOCK), jnp.float32)
    s_ref[NULL] = jnp.zeros((SPEEDS, BLOCK), jnp.bfloat16)
    xs_ref[NULL] = jnp.full((8, BLOCK), 1e6, jnp.float32)
    ys_ref[NULL] = jnp.zeros((8, BLOCK), jnp.float32)
    b_ref[NULL] = jnp.zeros((SPEEDS, BLOCK), jnp.float32)

    freq = freq_ref[...]
    speed = 0.4 + 0.75 * lax.broadcasted_iota(jnp.int32, (SPEEDS, BLOCK), 0).astype(jnp.float32) / (SPEEDS - 1)
    lane = lax.broadcasted_iota(jnp.int32, (SPEEDS, BLOCK), 1)
    low_weight = jnp.where(lane < 5 * ROWS, 1.0, 2.0)
    high_weight = jnp.where(lane < 7 * ROWS, 2.0, 0.0)
    scale = freq * (-0.25 * 3.0 / (GRID * GRID)) / speed

    for i in range(LAG):
        note_ref[0, i] = 0
        note_ref[1, i] = NULL
        note_ref[2, i] = NULL
        note_ref[3, i] = 2

    def add_back(done, term):
        b_ref[note_ref[1, done]] += term[:, :BLOCK]
        b_ref[note_ref[2, done]] += term[:, BLOCK:]

    def back_term(done, tc, k_ref):
        slot = lax.rem((done + (2 * RING - LAG)) // 2, RING)
        rows = slice(tc * LANES, (tc + 1) * LANES)
        kernel = jnp.concatenate([k_ref[slot, 0, rows, :], k_ref[slot, 1, rows, :]], axis=1)
        return jnp.dot(a_ref[note_ref[0, done], tc], kernel, preferred_element_type=jnp.float32)

    def fore_strength(done):
        return jnp.concatenate([s_ref[note_ref[1, done + LAG - 1]], s_ref[note_ref[2, done + LAG - 1]]], axis=1)

    def fore_term(done, tc, k_ref, strength):
        slot = lax.rem((done + (2 * RING - 1)) // 2, RING)
        rows = slice(tc * LANES, (tc + 1) * LANES)
        kernel = jnp.concatenate([jnp.transpose(k_ref[slot, h, rows, :]) for h in range(2)], axis=0)
        term = jnp.dot(strength, kernel, preferred_element_type=jnp.float32)
        d_ref[note_ref[3, done + LAG - 1], tc] += term

    def respond(b):
        sums = []
        for tc in range(CHUNKS):
            coef = spread_ref[b, tc : tc + 1, :] * scale
            v_low = speed / (1.0 + d_ref[b % 2, tc, :, :BLOCK])
            v_high = speed / (1.0 + d_ref[b % 2, tc, :, BLOCK:])
            s_low = v_low * v_low
            s_high = v_high * v_high
            a_ref[b, tc, :, :BLOCK] = (coef * low_weight * (s_low * s_low)).astype(jnp.bfloat16)
            a_ref[b, tc, :, BLOCK:] = (coef * high_weight * (s_high * s_high)).astype(jnp.bfloat16)
            total = low_weight * (s_low * v_low) + high_weight * (s_high * v_high)
            sums.append(total)
        for shift in (64, 32, 16):
            upper = (lane & shift) != 0
            half = len(sums) // 2
            merged = []
            for low, high in zip(sums[:half], sums[half:]):
                other = jnp.where(upper, low, high)
                moved = pltpu.roll(other, shift, 1)
                if shift != 64:
                    moved = jnp.where(upper, moved, pltpu.roll(other, BLOCK - shift, 1))
                merged.append(jnp.where(upper, high, low) + moved)
            sums = merged
        cube = sums[0] * (1.0 / (GRID * GRID))
        axial = axial_ref[pl.ds(b, 1), :]
        power_coef = 4.0 * axial * (1.0 - axial) * (1.0 - axial)
        slope_coef = 4.0 * (1.0 - axial) * (1.0 - 3.0 * axial)
        power_ref[:, pl.ds(pl.multiple_of(b * BLOCK, BLOCK), BLOCK)] = power_coef * cube
        direct_ref[pl.ds(b, 1), :] = jnp.sum(freq * (slope_coef * cube), axis=0, keepdims=True)

    def one_block(b, first):
        own = REACH * BLKS + b
        xt_ref[...] = jnp.transpose(jnp.broadcast_to(xs_ref[own][0:1, :], (BLOCK, BLOCK)))
        yt_ref[...] = jnp.transpose(jnp.broadcast_to(ys_ref[own][0:1, :], (BLOCK, BLOCK)))
        d_ref[b % 2] = jnp.zeros((CHUNKS, SPEEDS, LANES), jnp.float32)
        count = pairs_ref[b]

        def forward(p, carry):
            q0 = index_ref[b, 2 * p]
            q1 = index_ref[b, 2 * p + 1]
            done = first + p
            slot = lax.rem(done // 2, RING)
            note_ref[0, done + LAG] = b
            note_ref[1, done + LAG] = q0
            note_ref[2, done + LAG] = q1
            note_ref[3, done + LAG] = b % 2
            sx = [jnp.concatenate([xs_ref[q]] * 2, axis=0) for q in (q0, q1)]
            sy = [jnp.concatenate([ys_ref[q]] * 2, axis=0) for q in (q0, q1)]
            zero = jnp.zeros((ROWS, BLOCK), jnp.bfloat16)
            def step(new_ref, old_ref):
                strength = fore_strength(done)
                terms = [None, None]
                for tc in range(CHUNKS):
                    part = back_term(done, tc, old_ref)
                    terms[tc % 2] = part if terms[tc % 2] is None else terms[tc % 2] + part
                    fore_term(done, tc, old_ref, strength)
                    tx = xt_ref[tc * ROWS : (tc + 1) * ROWS, :]
                    ty = yt_ref[tc * ROWS : (tc + 1) * ROWS, :]
                    for h in range(2):
                        tiles = wake_tiles(tx, ty, sx[h], sy[h])
                        new_ref[slot, h, tc * LANES : (tc + 1) * LANES, :] = jnp.concatenate([k.astype(jnp.bfloat16) for k in tiles] + [zero], axis=0)
                add_back(done, terms[0] + terms[1])

            @pl.when(done % 2 == 0)
            def _():
                step(k0_ref, k1_ref)

            @pl.when(done % 2 == 1)
            def _():
                step(k1_ref, k0_ref)

            @pl.when((p == 0) & (b > 0))
            def _():
                respond(b - 1)

            return carry

        lax.fori_loop(0, count, forward, 0)

        return first + count

    total = lax.fori_loop(0, BLKS, one_block, 0)

    def finish(old_ref):
        strength = fore_strength(total)
        for tc in range(CHUNKS):
            fore_term(total, tc, old_ref, strength)

    @pl.when(total % 2 == 0)
    def _():
        finish(k1_ref)

    @pl.when(total % 2 == 1)
    def _():
        finish(k0_ref)

    respond(BLKS - 1)

    def backward(done, carry):
        def step(old_ref):
            term = back_term(done, 0, old_ref)
            for tc in range(1, CHUNKS):
                term = term + back_term(done, tc, old_ref)
            add_back(done, term)

        @pl.when(done % 2 == 0)
        def _():
            step(k1_ref)

        @pl.when(done % 2 == 1)
        def _():
            step(k0_ref)

        return carry

    lax.fori_loop(total, total + LAG, backward, 0)
    for o in range(PIECES):
        rows = []
        for blk in range(BLKS):
            strength = pieces[o][blk * SPEEDS : (blk + 1) * SPEEDS, :]
            rows.append(jnp.sum(freq * strength * b_ref[o * BLKS + blk], axis=0, keepdims=True))
        g_ref[GROUP - 1 + jnp.where(place_ref[1] == 0, o, PIECES - 1 - o)] = jnp.concatenate(rows, axis=0)
    for o in list(range(GROUP - 1)) + list(range(GROUP - 1 + PIECES, 2 * GROUP + PIECES - 2)):
        g_ref[o] = jnp.zeros((BLKS, BLOCK), jnp.float32)
    place = place_ref[0]
    for i in range(GROUP):
        first = i - place + GROUP - 1
        send_ref[i, 0] = g_ref[first + REACH]
        if i < REACH:
            send_ref[i, 1] = g_ref[first]
        elif i >= GROUP - REACH:
            send_ref[i, 1] = g_ref[first + 2 * REACH]
        else:
            send_ref[i, 1] = jnp.zeros((BLKS, BLOCK), jnp.float32)


def farm(index, pairs, place, pieces, axial, spread, freq):
    f32 = jnp.float32
    smem = pl.BlockSpec(memory_space=pltpu.SMEM)
    vmem = pl.BlockSpec(memory_space=pltpu.VMEM)
    piece = jax.ShapeDtypeStruct((BLKS, BLOCK), f32)
    return pl.pallas_call(
        farm_kernel,
        name="farm",
        out_shape=(jax.ShapeDtypeStruct((SPEEDS, BLKS * BLOCK), f32), piece, jax.ShapeDtypeStruct((GROUP, 2, BLKS, BLOCK), f32)),
        in_specs=[smem, smem, smem] + [vmem] * (PIECES + 3),
        out_specs=(vmem,) * 3,
        scratch_shapes=[
            pltpu.VMEM((SOURCES + 1, SPEEDS, BLOCK), jnp.bfloat16),
            pltpu.VMEM((SOURCES + 1, 8, BLOCK), f32),
            pltpu.VMEM((SOURCES + 1, 8, BLOCK), f32),
            pltpu.VMEM((BLOCK, BLOCK), f32),
            pltpu.VMEM((BLOCK, BLOCK), f32),
            pltpu.VMEM((3, CHUNKS, SPEEDS, LANES), f32),
            pltpu.VMEM((BLKS, CHUNKS, SPEEDS, LANES), jnp.bfloat16),
            pltpu.VMEM((RING, 2, CHUNKS * LANES, BLOCK), jnp.bfloat16),
            pltpu.VMEM((RING, 2, CHUNKS * LANES, BLOCK), jnp.bfloat16),
            pltpu.VMEM((SOURCES + 1, SPEEDS, BLOCK), f32),
            pltpu.VMEM((2 * GROUP + PIECES - 2, BLKS, BLOCK), f32),
            pltpu.SMEM((4, BLKS * PAIRS // 2 + LAG), jnp.int32),
        ],
        compiler_params=pltpu.CompilerParams(vmem_limit_bytes=32 << 20),
        cost_estimate=pl.CostEstimate(flops=2 * 64 * 128 * 2048 * 16 * 2, bytes_accessed=4 << 20, transcendentals=0),
    )(index, pairs, place, *pieces, axial, spread, freq)


def body(axial, thrust_weight, xdown, ycross, freq, upstream, counts):
    position = lax.axis_index("pt")
    lowest = (position - REACH) * BLKS
    strength = (axial[None, :] * thrust_weight[0]).reshape(SPEEDS, BLKS, BLOCK)
    strength = jnp.transpose(strength, (1, 0, 2)).reshape(BLKS * SPEEDS, BLOCK)
    packed = jnp.concatenate([strength, xdown[0].reshape(BLKS, BLOCK), ycross[0].reshape(BLKS, BLOCK)], axis=0)
    length = lax.axis_size("pt")
    core = position % 2
    swap = [(i, i ^ 1) for i in range(length)]
    hops = [[(i, i + by if i % 2 == up else i - by) for i in range(length)] for by, up in ((1, 1), (2, 0), (3, 1))]
    hops = [[(i, j) for i, j in pairs if 0 <= j < length] for pairs in hops]
    near, middle, far = [lax.ppermute(packed, "pt", pairs) for pairs in hops]
    turned = [lax.ppermute(value, "pt", swap) for value in (packed, near, middle)]
    pieces = [far, middle, near, packed] + turned
    slots = lax.broadcasted_iota(jnp.int32, (BLKS, PAIRS), 1)
    local = upstream[0] - lowest
    local = jnp.where(core == 0, local, (PIECES - 1) * BLKS - local + 2 * (local % BLKS))
    index = jnp.where(slots < counts[0][:, None], local, NULL)
    pairs = (counts[0] + 1) // 2
    axial_rows = axial.reshape(BLKS, BLOCK)
    power_coef = 4.0 * axial_rows * (1.0 - axial_rows) ** 2
    spread = jnp.broadcast_to(power_coef.reshape(BLKS, CHUNKS, 1, ROWS), (BLKS, CHUNKS, BLOCK // ROWS, ROWS)).reshape(BLKS, CHUNKS, BLOCK)
    freq_wide = jnp.broadcast_to(freq[0][:, None], (SPEEDS, BLOCK))
    place = jnp.stack([position % GROUP, core])
    power, direct, send = farm(index, pairs, place, pieces, axial_rows, spread, freq_wide)
    groups = [list(range(a, a + GROUP)) for a in range(0, length, GROUP)]
    arrived = jnp.sum(lax.all_to_all(send, "pt", 0, 0, axis_index_groups=groups), axis=0)
    across = []
    for a in range(GROUP, length, GROUP):
        for i in range(REACH):
            across += [(a - REACH + i, a + i), (a + i, a - REACH + i)]
    total = arrived[0] + lax.ppermute(arrived[1], "pt", across)
    gradient = direct + total / axial_rows
    spread_out = jnp.broadcast_to(gradient[None], (lax.axis_size("dir"),) + gradient.shape)
    gradient = jnp.sum(lax.all_to_all(spread_out, "dir", 0, 0), axis=0)
    return power[None], gradient.reshape(-1)


def solution(mesh):
    placed = (
        P("pt"),
        P("dir", None, "pt"),
        P("dir", "pt"),
        P("dir", "pt"),
        P("dir", None),
        P("dir", "pt", None),
        P("dir", "pt"),
    )
    return jax.shard_map(
        body, mesh=mesh, in_specs=placed, out_specs=(P("dir", None, "pt"), P("pt")), check_vma=False
    )
```

```python
import functools
import math
import jax
import jax.numpy as jnp
from jax import lax
from jax.experimental import pallas as pl
from jax.experimental.pallas import tpu as pltpu
from jax.sharding import PartitionSpec as P

BLOCK = 128
BLKS = 8
GRID = 5
SPEEDS = 16
REACH = 3
PIECES = 2 * REACH + 1
GROUP = 8
SOURCES = PIECES * BLKS
NULL = SOURCES
PAIRS = 16
LAG = 9
RING = 8
ROWS = 16
CHUNKS = BLOCK // ROWS
LANES = 16 * ROWS
LOG2E = math.log2(math.e)
Y_SCALE = 5.0
STEP = 0.2 * math.sqrt(2.0 * LOG2E)
WIDEN = 0.06 / LOG2E


def wake_tiles(target_x, target_y, source_x, source_y):
    behind = jnp.minimum(source_x - target_x, 0.0)
    ratio = 1.0 / ((1.0 / STEP) - (WIDEN / STEP) * behind)
    minus_q = -(ratio * ratio)
    fall = jnp.exp2(behind) * (1.0 / (STEP * STEP)) - (1.0 / (STEP * STEP))
    lateral = target_y - source_y
    lateral_q = lateral * minus_q
    centre = (minus_q * fall) * jnp.exp2(lateral * lateral_q)
    tilt = lateral_q + lateral_q
    u1 = jnp.exp2(minus_q)
    right = jnp.exp2(minus_q + tilt)
    left = jnp.exp2(minus_q - tilt)
    u2 = u1 * u1
    u4 = u2 * u2
    right1 = centre * right
    left1 = centre * left
    right2 = right1 * (right * u2)
    left2 = left1 * (left * u2)
    base = [left2, left1, centre, right1, right2]
    return base + [k * u1 for k in base] + [k * u4 for k in base]


def farm_kernel(index_ref, pairs_ref, place_ref, *refs):
    pieces = refs[:PIECES]
    axial_ref, spread_ref, freq_ref = refs[PIECES : PIECES + 3]
    power_ref, direct_ref, send_ref = refs[PIECES + 3 : PIECES + 6]
    s_ref, xs_ref, ys_ref, xt_ref, yt_ref, d_ref, a_ref, k0_ref, k1_ref, b_ref, g_ref, note_ref = refs[PIECES + 6 :]

    for o in range(PIECES):
        for blk in range(BLKS):
            q = o * BLKS + blk
            s_ref[q] = (pieces[o][blk * SPEEDS : (blk + 1) * SPEEDS, :] * 0.25).astype(jnp.bfloat16)
            row = SPEEDS * BLKS + blk
            xs_ref[q] = jnp.broadcast_to(pieces[o][row : row + 1, :] * LOG2E, (8, BLOCK))
            row = row + BLKS
            ys_ref[q] = jnp.broadcast_to(pieces[o][row : row + 1, :] * Y_SCALE, (8, BLOCK))
            b_ref[q] = jnp.zeros((SPEEDS, BLOCK), jnp.float32)
    s_ref[NULL] = jnp.zeros((SPEEDS, BLOCK), jnp.bfloat16)
    xs_ref[NULL] = jnp.full((8, BLOCK), 1e6, jnp.float32)
    ys_ref[NULL] = jnp.zeros((8, BLOCK), jnp.float32)
    b_ref[NULL] = jnp.zeros((SPEEDS, BLOCK), jnp.float32)

    freq = freq_ref[...]
    speed = 0.4 + 0.75 * lax.broadcasted_iota(jnp.int32, (SPEEDS, BLOCK), 0).astype(jnp.float32) / (SPEEDS - 1)
    lane = lax.broadcasted_iota(jnp.int32, (SPEEDS, BLOCK), 1)
    low_weight = jnp.where(lane < 5 * ROWS, 1.0, 2.0)
    high_weight = jnp.where(lane < 7 * ROWS, 2.0, 0.0)
    scale = freq * (-0.25 * 3.0 / (GRID * GRID)) / speed

    for i in range(LAG):
        note_ref[0, i] = 0
        note_ref[1, i] = NULL
        note_ref[2, i] = NULL
        note_ref[3, i] = 2

    def add_back(done, term):
        b_ref[note_ref[1, done]] += term[:, :BLOCK]
        b_ref[note_ref[2, done]] += term[:, BLOCK:]

    def back_term(done, tc, k_ref):
        slot = lax.rem((done + (2 * RING - LAG)) // 2, RING)
        rows = slice(tc * LANES, (tc + 1) * LANES)
        kernel = jnp.concatenate([k_ref[slot, 0, rows, :], k_ref[slot, 1, rows, :]], axis=1)
        return jnp.dot(a_ref[note_ref[0, done], tc], kernel, preferred_element_type=jnp.float32)

    def fore_strength(done):
        return jnp.concatenate([s_ref[note_ref[1, done + LAG - 1]], s_ref[note_ref[2, done + LAG - 1]]], axis=1)

    def fore_term(done, tc, k_ref, strength):
        slot = lax.rem((done + (2 * RING - 1)) // 2, RING)
        rows = slice(tc * LANES, (tc + 1) * LANES)
        kernel = jnp.concatenate([jnp.transpose(k_ref[slot, h, rows, :]) for h in range(2)], axis=0)
        term = jnp.dot(strength, kernel, preferred_element_type=jnp.float32)
        d_ref[note_ref[3, done + LAG - 1], tc] += term

    def respond(b):
        sums = []
        for tc in range(CHUNKS):
            coef = spread_ref[b, tc : tc + 1, :] * scale
            v_low = speed / (1.0 + d_ref[b % 2, tc, :, :BLOCK])
            v_high = speed / (1.0 + d_ref[b % 2, tc, :, BLOCK:])
            s_low = v_low * v_low
            s_high = v_high * v_high
            a_ref[b, tc, :, :BLOCK] = (coef * low_weight * (s_low * s_low)).astype(jnp.bfloat16)
            a_ref[b, tc, :, BLOCK:] = (coef * high_weight * (s_high * s_high)).astype(jnp.bfloat16)
            total = low_weight * (s_low * v_low) + high_weight * (s_high * v_high)
            sums.append(total)
        for shift in (64, 32, 16):
            upper = (lane & shift) != 0
            half = len(sums) // 2
            merged = []
            for low, high in zip(sums[:half], sums[half:]):
                other = jnp.where(upper, low, high)
                moved = pltpu.roll(other, shift, 1)
                if shift != 64:
                    moved = jnp.where(upper, moved, pltpu.roll(other, BLOCK - shift, 1))
                merged.append(jnp.where(upper, high, low) + moved)
            sums = merged
        cube = sums[0] * (1.0 / (GRID * GRID))
        axial = axial_ref[pl.ds(b, 1), :]
        power_coef = 4.0 * axial * (1.0 - axial) * (1.0 - axial)
        slope_coef = 4.0 * (1.0 - axial) * (1.0 - 3.0 * axial)
        power_ref[:, pl.ds(pl.multiple_of(b * BLOCK, BLOCK), BLOCK)] = power_coef * cube
        direct_ref[pl.ds(b, 1), :] = jnp.sum(freq * (slope_coef * cube), axis=0, keepdims=True)

    def one_block(b, first):
        own = REACH * BLKS + b
        xt_ref[...] = jnp.transpose(jnp.broadcast_to(xs_ref[own][0:1, :], (BLOCK, BLOCK)))
        yt_ref[...] = jnp.transpose(jnp.broadcast_to(ys_ref[own][0:1, :], (BLOCK, BLOCK)))
        d_ref[b % 2] = jnp.zeros((CHUNKS, SPEEDS, LANES), jnp.float32)
        count = pairs_ref[b]

        def forward(p, carry):
            q0 = index_ref[b, 2 * p]
            q1 = index_ref[b, 2 * p + 1]
            done = first + p
            slot = lax.rem(done // 2, RING)
            note_ref[0, done + LAG] = b
            note_ref[1, done + LAG] = q0
            note_ref[2, done + LAG] = q1
            note_ref[3, done + LAG] = b % 2
            sx = [jnp.concatenate([xs_ref[q]] * 2, axis=0) for q in (q0, q1)]
            sy = [jnp.concatenate([ys_ref[q]] * 2, axis=0) for q in (q0, q1)]
            zero = jnp.zeros((ROWS, BLOCK), jnp.bfloat16)
            def step(new_ref, old_ref):
                strength = fore_strength(done)
                terms = [None, None]
                for tc in range(CHUNKS):
                    fore_term(done, tc, old_ref, strength)
                    part = back_term(done, tc, old_ref)
                    terms[tc % 2] = part if terms[tc % 2] is None else terms[tc % 2] + part
                    tx = xt_ref[tc * ROWS : (tc + 1) * ROWS, :]
                    ty = yt_ref[tc * ROWS : (tc + 1) * ROWS, :]
                    for h in range(2):
                        tiles = wake_tiles(tx, ty, sx[h], sy[h])
                        new_ref[slot, h, tc * LANES : (tc + 1) * LANES, :] = jnp.concatenate([k.astype(jnp.bfloat16) for k in tiles] + [zero], axis=0)
                add_back(done, terms[0] + terms[1])

            @pl.when(done % 2 == 0)
            def _():
                step(k0_ref, k1_ref)

            @pl.when(done % 2 == 1)
            def _():
                step(k1_ref, k0_ref)

            @pl.when((p == 0) & (b > 0))
            def _():
                respond(b - 1)

            return carry

        lax.fori_loop(0, count, forward, 0)

        return first + count

    total = lax.fori_loop(0, BLKS, one_block, 0)

    def finish(old_ref):
        strength = fore_strength(total)
        for tc in range(CHUNKS):
            fore_term(total, tc, old_ref, strength)

    @pl.when(total % 2 == 0)
    def _():
        finish(k1_ref)

    @pl.when(total % 2 == 1)
    def _():
        finish(k0_ref)

    respond(BLKS - 1)

    def backward(done, carry):
        def step(old_ref):
            term = back_term(done, 0, old_ref)
            for tc in range(1, CHUNKS):
                term = term + back_term(done, tc, old_ref)
            add_back(done, term)

        @pl.when(done % 2 == 0)
        def _():
            step(k1_ref)

        @pl.when(done % 2 == 1)
        def _():
            step(k0_ref)

        return carry

    lax.fori_loop(total, total + LAG, backward, 0)
    for o in range(PIECES):
        rows = []
        for blk in range(BLKS):
            strength = pieces[o][blk * SPEEDS : (blk + 1) * SPEEDS, :]
            rows.append(jnp.sum(freq * strength * b_ref[o * BLKS + blk], axis=0, keepdims=True))
        g_ref[GROUP - 1 + jnp.where(place_ref[1] == 0, o, PIECES - 1 - o)] = jnp.concatenate(rows, axis=0)
    for o in list(range(GROUP - 1)) + list(range(GROUP - 1 + PIECES, 2 * GROUP + PIECES - 2)):
        g_ref[o] = jnp.zeros((BLKS, BLOCK), jnp.float32)
    place = place_ref[0]
    for i in range(GROUP):
        first = i - place + GROUP - 1
        send_ref[i, 0] = g_ref[first + REACH]
        if i < REACH:
            send_ref[i, 1] = g_ref[first]
        elif i >= GROUP - REACH:
            send_ref[i, 1] = g_ref[first + 2 * REACH]
        else:
            send_ref[i, 1] = jnp.zeros((BLKS, BLOCK), jnp.float32)


def farm(index, pairs, place, pieces, axial, spread, freq):
    f32 = jnp.float32
    smem = pl.BlockSpec(memory_space=pltpu.SMEM)
    vmem = pl.BlockSpec(memory_space=pltpu.VMEM)
    piece = jax.ShapeDtypeStruct((BLKS, BLOCK), f32)
    return pl.pallas_call(
        farm_kernel,
        name="farm",
        out_shape=(jax.ShapeDtypeStruct((SPEEDS, BLKS * BLOCK), f32), piece, jax.ShapeDtypeStruct((GROUP, 2, BLKS, BLOCK), f32)),
        in_specs=[smem, smem, smem] + [vmem] * (PIECES + 3),
        out_specs=(vmem,) * 3,
        scratch_shapes=[
            pltpu.VMEM((SOURCES + 1, SPEEDS, BLOCK), jnp.bfloat16),
            pltpu.VMEM((SOURCES + 1, 8, BLOCK), f32),
            pltpu.VMEM((SOURCES + 1, 8, BLOCK), f32),
            pltpu.VMEM((BLOCK, BLOCK), f32),
            pltpu.VMEM((BLOCK, BLOCK), f32),
            pltpu.VMEM((3, CHUNKS, SPEEDS, LANES), f32),
            pltpu.VMEM((BLKS, CHUNKS, SPEEDS, LANES), jnp.bfloat16),
            pltpu.VMEM((RING, 2, CHUNKS * LANES, BLOCK), jnp.bfloat16),
            pltpu.VMEM((RING, 2, CHUNKS * LANES, BLOCK), jnp.bfloat16),
            pltpu.VMEM((SOURCES + 1, SPEEDS, BLOCK), f32),
            pltpu.VMEM((2 * GROUP + PIECES - 2, BLKS, BLOCK), f32),
            pltpu.SMEM((4, BLKS * PAIRS // 2 + LAG), jnp.int32),
        ],
        compiler_params=pltpu.CompilerParams(vmem_limit_bytes=32 << 20),
        cost_estimate=pl.CostEstimate(flops=2 * 64 * 128 * 2048 * 16 * 2, bytes_accessed=4 << 20, transcendentals=0),
    )(index, pairs, place, *pieces, axial, spread, freq)


def body(axial, thrust_weight, xdown, ycross, freq, upstream, counts):
    position = lax.axis_index("pt")
    lowest = (position - REACH) * BLKS
    strength = (axial[None, :] * thrust_weight[0]).reshape(SPEEDS, BLKS, BLOCK)
    strength = jnp.transpose(strength, (1, 0, 2)).reshape(BLKS * SPEEDS, BLOCK)
    packed = jnp.concatenate([strength, xdown[0].reshape(BLKS, BLOCK), ycross[0].reshape(BLKS, BLOCK)], axis=0)
    length = lax.axis_size("pt")
    core = position % 2
    swap = [(i, i ^ 1) for i in range(length)]
    hops = [[(i, i + by if i % 2 == up else i - by) for i in range(length)] for by, up in ((1, 1), (2, 0), (3, 1))]
    hops = [[(i, j) for i, j in pairs if 0 <= j < length] for pairs in hops]
    near, middle, far = [lax.ppermute(packed, "pt", pairs) for pairs in hops]
    turned = [lax.ppermute(value, "pt", swap) for value in (packed, near, middle)]
    pieces = [far, middle, near, packed] + turned
    slots = lax.broadcasted_iota(jnp.int32, (BLKS, PAIRS), 1)
    local = upstream[0] - lowest
    local = jnp.where(core == 0, local, (PIECES - 1) * BLKS - local + 2 * (local % BLKS))
    index = jnp.where(slots < counts[0][:, None], local, NULL)
    pairs = (counts[0] + 1) // 2
    axial_rows = axial.reshape(BLKS, BLOCK)
    power_coef = 4.0 * axial_rows * (1.0 - axial_rows) ** 2
    spread = jnp.broadcast_to(power_coef.reshape(BLKS, CHUNKS, 1, ROWS), (BLKS, CHUNKS, BLOCK // ROWS, ROWS)).reshape(BLKS, CHUNKS, BLOCK)
    freq_wide = jnp.broadcast_to(freq[0][:, None], (SPEEDS, BLOCK))
    place = jnp.stack([position % GROUP, core])
    power, direct, send = farm(index, pairs, place, pieces, axial_rows, spread, freq_wide)
    groups = [list(range(a, a + GROUP)) for a in range(0, length, GROUP)]
    arrived = jnp.sum(lax.all_to_all(send, "pt", 0, 0, axis_index_groups=groups), axis=0)
    across = []
    for a in range(GROUP, length, GROUP):
        for i in range(REACH):
            across += [(a - REACH + i, a + i), (a + i, a - REACH + i)]
    total = arrived[0] + lax.ppermute(arrived[1], "pt", across)
    gradient = direct + total / axial_rows
    spread_out = jnp.broadcast_to(gradient[None], (lax.axis_size("dir"),) + gradient.shape)
    gradient = jnp.sum(lax.all_to_all(spread_out, "dir", 0, 0), axis=0)
    return power[None], gradient.reshape(-1)


def solution(mesh):
    placed = (
        P("pt"),
        P("dir", None, "pt"),
        P("dir", "pt"),
        P("dir", "pt"),
        P("dir", None),
        P("dir", "pt", None),
        P("dir", "pt"),
    )
    return jax.shard_map(
        body, mesh=mesh, in_specs=placed, out_specs=(P("dir", None, "pt"), P("pt")), check_vma=False
    )
```
